128 devices in a mesh: dp: 16 (over x, y_lo, core), tensor: 8 (over z, y_hi).
Axes of the slice: x: 4, y: 4 (y_hi: 2, y_lo: 2; y = y_hi * 2 + y_lo), z: 4, core: 2. Of those that a mesh axis runs over, the one named last changes fastest.
Arguments:
- tokens: bfloat16 [1024, 8192], P(None, 'dp'), may hold values from -6 to 6
- cotangent: bfloat16 [1024, 8192], P(None, 'dp'), may hold values from -6 to 6
- gate_weight: bfloat16 [8192, 14336], P('dp', 'tensor'), may hold values from -0.0625 to 0.0625
- up_weight: bfloat16 [8192, 14336], P('dp', 'tensor'), may hold values from -0.0625 to 0.0625
- down_weight: bfloat16 [14336, 8192], P('tensor', 'dp'), may hold values from -0.0625 to 0.0625
- kept_blocks: int32 [56], replicated, may hold values from 0 to 111, as said below
Outputs:
- ffn_output: bfloat16 [1024, 8192], P('tensor', 'dp')
- input_gradient: bfloat16 [1024, 8192], P('tensor', 'dp')
- gate_weight_grad: bfloat16 [8192, 14336], P('dp', 'tensor')
- up_weight_grad: bfloat16 [8192, 14336], P('dp', 'tensor')
- down_weight_grad: bfloat16 [14336, 8192], P('tensor', 'dp')
The draws below stay inside these ranges and needn't reach their ends.
Inputs may be any that keep to these rules, and one draw needn't show every extreme that they name: kept_blocks is strictly increasing. Shard t of the tensor axis stores blocks t * 14 to (t + 1) * 14 - 1; shards 2 s and 2 s + 1 together hold exactly 14 kept blocks, each shard at most 11, and in every draw some shard holds exactly 11.
All inputs are finite; a program needn't handle non-finite values.
Results may differ from the reference program's by a relative error of at most 0.005.
Values may be sent and summed in bfloat16 or wider, within the bound.
No kernel may reach another device: no remote copies, remote signals or barrier semaphores. Data moves between devices by JAX's collectives and lax.ppermute only.
A program may use at most 128 MiB of HBM per device.

```python
import jax
import jax.numpy as jnp

D = 8192
BLK = 128
OB_DEV = 14
KB_DEV = 7
MAXK = 11
TOKENS = 1024
FFO = 14336
KEPT = 56
FF = 7168


def shuffle_one(subkey):
    return jax.random.permutation(subkey, OB_DEV)


def draw_kept_blocks(key, part):
    shards = FFO // (BLK * OB_DEV)
    pair_count = shards // 2
    key_scatter_layout, key_full, key_side, key_pick = jax.random.split(jax.random.fold_in(key, 11), 4)
    most_extra = MAXK - KB_DEV
    spread_by = jax.random.randint(key_scatter_layout, (pair_count,), 0, most_extra + 1)
    full_pair = jax.random.randint(key_full, (), 0, pair_count)
    spread_by = jnp.where(jnp.arange(pair_count) == full_pair, most_extra, spread_by)
    heavy_side = jax.random.randint(key_side, (pair_count,), 0, 2) * 2 - 1
    counts = jnp.stack([KB_DEV + heavy_side * spread_by, KB_DEV - heavy_side * spread_by], axis=1).reshape(shards)
    shuffled = jax.vmap(shuffle_one)(jax.random.split(key_pick, shards))
    chosen = (shuffled < counts[:, None]).reshape(-1)
    return jnp.nonzero(chosen, size=KEPT, fill_value=0)[0].astype(jnp.int32)


def block_levels(own_key, extent, pieces, smallest, top_value):
    def one(position, parts):
        heights = jax.random.uniform(jax.random.fold_in(jax.random.fold_in(own_key, 6), position), (parts,), jnp.float32, smallest / len(pieces), top_value / len(pieces))
        return jnp.repeat(jnp.exp(heights), extent[position] // parts).reshape((-1,) + (1,) * (len(extent) - position - 1))

    level = one(*pieces[0])
    for cut in pieces[1:]:
        level = level * one(*cut)
    return level


def centred(key, dims, width, most, cuts=(), kind=jnp.bfloat16):
    loudness = block_levels(key, dims, cuts, -0.22, 0.18) if cuts else 1.0
    drawn = jax.random.normal(key, dims, jnp.float32) * width * loudness
    return jnp.minimum(jnp.maximum(drawn, -most), most).astype(kind)


def setup_inputs(seed: int = 0) -> dict:
    keys = jax.random.split(jax.random.key(seed), 7)
    tokens = centred(keys[0], (TOKENS, D), 1.0, 6.0, ((1, 16),))
    cotangent = centred(keys[1], (TOKENS, D), 1.0, 6.0, ((1, 16),))
    gate_weight = centred(keys[2], (D, FFO), D ** -0.5, 0.0625, ((0, 16), (1, 8)))
    up_weight = centred(keys[3], (D, FFO), D ** -0.5, 0.0625, ((0, 16), (1, 8)))
    down_weight = centred(keys[4], (FFO, D), FF ** -0.5, 0.0625, ((0, 8), (1, 16)))
    kept_blocks = draw_kept_blocks(jax.random.fold_in(keys[6], 71), 0)
    return {"tokens": tokens, "cotangent": cotangent, "gate_weight": gate_weight, "up_weight": up_weight, "down_weight": down_weight, "kept_blocks": kept_blocks}


def reference(tokens, cotangent, gate_weight, up_weight, down_weight, kept_blocks):
    columns = (kept_blocks[:, None] * BLK + jnp.arange(BLK, dtype=jnp.int32)[None, :]).reshape(-1).astype(jnp.int32)
    w_gate = jnp.take(gate_weight, columns, axis=1)
    w_up = jnp.take(up_weight, columns, axis=1)
    w_down = jnp.take(down_weight, columns, axis=0)
    gate_value = jnp.dot(tokens, w_gate, preferred_element_type=jnp.float32)
    up_value = jnp.dot(tokens, w_up, preferred_element_type=jnp.float32)
    sigmoid_gate = jax.nn.sigmoid(gate_value)
    hidden_value = (gate_value * sigmoid_gate * up_value).astype(jnp.bfloat16)
    ffn_output = jnp.dot(hidden_value, w_down, preferred_element_type=jnp.float32).astype(jnp.bfloat16)
    hidden_delta = jnp.dot(cotangent, w_down.T, preferred_element_type=jnp.float32)
    gate_delta = (hidden_delta * up_value * sigmoid_gate * (1.0 + gate_value * (1.0 - sigmoid_gate))).astype(jnp.bfloat16)
    up_delta = (hidden_delta * gate_value * sigmoid_gate).astype(jnp.bfloat16)
    input_gradient = (jnp.dot(gate_delta, w_gate.T, preferred_element_type=jnp.float32)
                  + jnp.dot(up_delta, w_up.T, preferred_element_type=jnp.float32)).astype(jnp.bfloat16)
    gate_kept = jnp.dot(tokens.T, gate_delta, preferred_element_type=jnp.float32).astype(jnp.bfloat16)
    up_kept = jnp.dot(tokens.T, up_delta, preferred_element_type=jnp.float32).astype(jnp.bfloat16)
    down_kept = jnp.dot(hidden_value.T, cotangent, preferred_element_type=jnp.float32).astype(jnp.bfloat16)
    gate_weight_grad = jnp.zeros(gate_weight.shape, jnp.bfloat16).at[:, columns].set(gate_kept)
    up_weight_grad = jnp.zeros(up_weight.shape, jnp.bfloat16).at[:, columns].set(up_kept)
    down_weight_grad = jnp.zeros(down_weight.shape, jnp.bfloat16).at[columns, :].set(down_kept)
    return ffn_output, input_gradient, gate_weight_grad, up_weight_grad, down_weight_grad
```

```python
import functools

import jax
import jax.numpy as jnp
from jax import lax
from jax.experimental import pallas as pl
from jax.experimental.pallas import tpu as pltpu
from jax.sharding import PartitionSpec as P

BLK = 128
HALF = 6
UNITS = HALF * BLK
ROWS = 128
BF = jnp.bfloat16
F32 = jnp.float32
VM = pl.BlockSpec(memory_space=pltpu.VMEM)
SM = pl.BlockSpec(memory_space=pltpu.SMEM)
ANY = pl.BlockSpec(memory_space=pl.ANY)


FLIP_DP = {"a": 4, "b": 12, "y": 2, "c": 1}
FLIP_TP = {"a": 2, "b": 6, "y": 1}
GATE, UP, DOWN = "aby", "bya", "yab"


def swap(value, direction):
    flip = FLIP_DP[direction]
    return lax.ppermute(value, "dp", [(i, i ^ flip) for i in range(16)])


def swap_tensor(value, direction):
    flip = FLIP_TP[direction]
    return lax.ppermute(value, "tensor", [(i, i ^ flip) for i in range(8)])


def square(v):
    return (v ^ (v >> 1)) & 1, v >> 1


def place_dp(meta_ref):
    d = meta_ref[0]
    a, b = square(d >> 2)
    return {"a": a, "b": b, "y": (d >> 1) & 1}


def place_tensor(meta_ref):
    t = meta_ref[1]
    a, b = square(t >> 1)
    return {"a": a, "b": b, "y": t & 1}


def bits(order, i):
    return {order[0]: (i >> 2) & 1, order[1]: (i >> 1) & 1, order[2]: i & 1}


def xor(p, q):
    return {k: p[k] ^ q[k] for k in "aby"}


def number(order, p):
    return p[order[0]] * 4 + p[order[1]] * 2 + p[order[2]]


def token_chunk(p):
    return p["b"] * 4 + (p["a"] ^ p["b"]) * 2 + p["y"]


def rows(ref, chunk):
    return ref[pl.ds(pl.multiple_of(chunk * ROWS, ROWS), ROWS), :]


def call(kernel, outs, specs, args, scratch=(), flops=0, nbytes=0, out_specs=None):
    return pl.pallas_call(
        kernel,
        out_shape=outs,
        in_specs=specs,
        out_specs=out_specs if out_specs is not None else jax.tree.map(lambda _: VM, outs),
        scratch_shapes=list(scratch),
        cost_estimate=pl.CostEstimate(flops=flops, bytes_accessed=nbytes, transcendentals=0),
        compiler_params=pltpu.CompilerParams(vmem_limit_bytes=50 * 2**20),
    )(*args)


def shape(*dims, dtype=BF):
    return jax.ShapeDtypeStruct(dims, dtype)


def slots(meta_ref, kept_ref, owned):
    first = meta_ref[1] * owned

    def step(k, carry):
        start, end = carry
        block = kept_ref[k]
        return start + (block < first).astype(jnp.int32), end + (block < first + owned).astype(jnp.int32)

    start, end = lax.fori_loop(0, kept_ref.shape[0], step, (jnp.int32(0), jnp.int32(0)))
    return first, start, end - start


def gather_kernel(owned, other, meta_ref, kept_ref, gate, up, down, gate_out, up_out, down_out, sem):
    first, start, count = slots(meta_ref, kept_ref, owned)
    core = (meta_ref[0] & 1) ^ other

    def copies(k):
        slot = core * HALF + k
        live = slot < count
        at = jnp.minimum(start + slot, kept_ref.shape[0] - 1)
        block = jnp.where(live, kept_ref[at] - first, 0)
        here = pl.ds(k * BLK, BLK)
        there = pl.ds(pl.multiple_of(block * BLK, BLK), BLK)
        return live, [
            pltpu.make_async_copy(gate.at[:, there], gate_out.at[:, here], sem.at[k, 0]),
            pltpu.make_async_copy(up.at[:, there], up_out.at[:, here], sem.at[k, 1]),
            pltpu.make_async_copy(down.at[there, :], down_out.at[here, :], sem.at[k, 2]),
        ]

    for k in range(HALF):
        live, group = copies(k)

        @pl.when(live)
        def _():
            for c in group:
                c.start()

        @pl.when(jnp.logical_not(live))
        def _():
            gate_out[:, k * BLK : (k + 1) * BLK] = jnp.zeros((gate_out.shape[0], BLK), BF)
            up_out[:, k * BLK : (k + 1) * BLK] = jnp.zeros((up_out.shape[0], BLK), BF)
            down_out[k * BLK : (k + 1) * BLK, :] = jnp.zeros((BLK, down_out.shape[1]), BF)

    for k in range(HALF):
        live, group = copies(k)

        @pl.when(live)
        def _():
            for c in group:
                c.wait()


def scatter_kernel(owned, meta_ref, kept_ref, *refs):
    mine, theirs, outs, (zero_col, zero_row, sem) = refs[0:3], refs[3:6], refs[6:9], refs[9:12]
    first, start, count = slots(meta_ref, kept_ref, owned)
    core = meta_ref[0] & 1
    zero_col[...] = jnp.zeros_like(zero_col)
    zero_row[...] = jnp.zeros_like(zero_row)

    def step(block, slot):
        at = jnp.minimum(start + slot, kept_ref.shape[0] - 1)
        live = (slot < count) & (kept_ref[at] == first + block)
        from_core = (slot >= HALF).astype(jnp.int32)
        place = pl.ds(pl.multiple_of((slot - from_core * HALF) * BLK, BLK), BLK)
        there = pl.ds(pl.multiple_of(block * BLK, BLK), BLK)
        own = from_core == core
        to_gate, to_up, to_down = outs[0].at[:, there], outs[1].at[:, there], outs[2].at[there, :]

        @pl.when(live & own)
        def _():
            pltpu.make_async_copy(mine[0].at[:, place], to_gate, sem.at[0]).start()
            pltpu.make_async_copy(mine[1].at[:, place], to_up, sem.at[1]).start()
            pltpu.make_async_copy(mine[2].at[place, :], to_down, sem.at[2]).start()

        @pl.when(live & jnp.logical_not(own))
        def _():
            pltpu.make_async_copy(theirs[0].at[:, place], to_gate, sem.at[0]).start()
            pltpu.make_async_copy(theirs[1].at[:, place], to_up, sem.at[1]).start()
            pltpu.make_async_copy(theirs[2].at[place, :], to_down, sem.at[2]).start()

        @pl.when(jnp.logical_not(live))
        def _():
            pltpu.make_async_copy(zero_col, to_gate, sem.at[0]).start()
            pltpu.make_async_copy(zero_col, to_up, sem.at[1]).start()
            pltpu.make_async_copy(zero_row, to_down, sem.at[2]).start()

        return slot + live.astype(jnp.int32)

    lax.fori_loop(0, owned, step, jnp.int32(0))
    for i, out in enumerate(outs):
        pltpu.make_async_copy(out, out, sem.at[i]).wait()


def dot(left, right, dims):
    return lax.dot_general(left, right, ((dims[:1], dims[1:]), ((), ())), preferred_element_type=F32)


def forward_kernel(order, half, dims, meta_ref, mine, theirs, weight, weight_theirs, out, left, right):
    here = place_dp(meta_ref)
    for q in range(4):
        chunk = token_chunk(xor(bits(order, half * 4 + q), here))
        left[q * ROWS : (q + 1) * ROWS, :] = rows(mine, chunk)
        right[q * ROWS : (q + 1) * ROWS, :] = rows(theirs, chunk)
    for r in range(0, 512, 256):
        out[r : r + 256, :] = (
            dot(left[r : r + 256, :], weight[...], dims) + dot(right[r : r + 256, :], weight_theirs[...], dims)
        ).astype(out.dtype)


def forward(order, half, dims, meta, mine, theirs, weight, weight_theirs):
    features = mine.shape[1]
    return call(
        functools.partial(forward_kernel, order, half, dims),
        shape(512, UNITS, dtype=F32 if half == 0 else BF),
        [SM] + [VM] * 4,
        (meta, mine, theirs, weight, weight_theirs),
        [pltpu.VMEM((512, features), BF), pltpu.VMEM((512, features), BF)],
        flops=2 * 512 * 2 * features * UNITS,
        nbytes=6 * 2**20,
    )


def output_kernel(tail, orders, dims, meta_ref, *refs):
    n = len(orders)
    values, weights, out, held = refs[:n], refs[n : 2 * n], refs[2 * n], refs[2 * n + 1 :]
    here = xor(place_dp(meta_ref), place_tensor(meta_ref))
    for j in range(8):
        p = xor(bits(tail, j), here)
        for order, value, to in zip(orders, values, held):
            to[j * ROWS : (j + 1) * ROWS, :] = rows(value, number(order, p))

    def step(r, _):
        at = pl.ds(pl.multiple_of(r * 256, 256), 256)
        total = dot(held[0][at, :], weights[0][...], dims)
        for v, w in zip(held[1:], weights[1:]):
            total = total + dot(v[at, :], w[...], dims)
        out[at, :] = total.astype(out.dtype)
        return 0

    lax.fori_loop(0, 4, step, 0)


def output(tail, orders, dims, dtype, meta, values, weights, features):
    return call(
        functools.partial(output_kernel, tail, orders, dims),
        shape(1024, features, dtype=dtype),
        [SM] + [VM] * (2 * len(orders)),
        (meta, *values, *weights),
        [pltpu.VMEM((1024, UNITS), BF)] * len(orders),
        flops=2 * 1024 * UNITS * features * len(orders),
        nbytes=6 * 2**20,
    )


def gradient_kernel(meta_ref, tokens, cotangent, hidden, gate_delta, up_delta, gate_out, up_out, down_out, held):
    here = place_dp(meta_ref)

    def arrange(order, source):
        for i in range(8):
            held[i * ROWS : (i + 1) * ROWS, :] = rows(source, token_chunk(xor(bits(order, i), here)))

    arrange(GATE, tokens)
    gate_out[...] = dot(held[...], gate_delta[...], (0, 0)).astype(BF)
    arrange(UP, tokens)
    up_out[...] = dot(held[...], up_delta[...], (0, 0)).astype(BF)
    arrange(DOWN, cotangent)
    down_out[...] = dot(hidden[...], held[...], (0, 0)).astype(BF)


def gradients(meta, tokens, cotangent, hidden, gate_delta, up_delta):
    features = tokens.shape[1]
    return call(
        gradient_kernel,
        (shape(features, UNITS), shape(features, UNITS), shape(UNITS, features)),
        [SM] + [VM] * 5,
        (meta, tokens, cotangent, hidden, gate_delta, up_delta),
        [pltpu.VMEM((1024, features), BF)],
        flops=3 * 2 * 1024 * UNITS * features,
        nbytes=9 * 2**20,
    )


def reduce_rest(total, order, send, types):
    for direction, dtype in zip(order, types):
        n = total.shape[0] // 2
        got = send(total[n:].astype(dtype), direction)
        total = total[:n] + got.astype(F32)
    return total


def gather_rows(value, order):
    for direction in reversed(order):
        value = jnp.concatenate([value, swap(value, direction)], axis=0)
    return value


def body(tokens, cotangent, gate_weight, up_weight, down_weight, kept_blocks):
    features = tokens.shape[1]
    owned = gate_weight.shape[1] // BLK
    meta = jnp.stack([lax.axis_index("dp"), lax.axis_index("tensor")]).astype(jnp.int32)

    tokens_o = swap(tokens, "c")
    cotangent_o = swap(cotangent, "c")

    def gather(other):
        return call(
            functools.partial(gather_kernel, owned, other),
            (shape(features, UNITS), shape(features, UNITS), shape(UNITS, features)),
            [SM, SM, ANY, ANY, ANY],
            (meta, kept_blocks, gate_weight, up_weight, down_weight),
            [pltpu.SemaphoreType.DMA((HALF, 3))],
            nbytes=5 * 2**20,
        )

    gate_send, up_send, down_send = gather(1)
    gate_o, up_o, down_o = swap(gate_send, "c"), swap(up_send, "c"), swap(down_send, "c")
    gate_w, up_w, down_w = gather(0)

    parts = (
        (GATE, (1, 0), tokens, tokens_o, gate_w, gate_o),
        (UP, (1, 0), tokens, tokens_o, up_w, up_o),
        (DOWN, (1, 1), cotangent, cotangent_o, down_w, down_o),
    )
    arrived = [swap(forward(order, 1, dims, meta, *rest), order[0]) for order, dims, *rest in parts]
    totals = []
    for (order, dims, *rest), got in zip(parts, arrived):
        total = forward(order, 0, dims, meta, *rest) + got.astype(F32)
        totals.append(reduce_rest(total, order[1:], swap, (BF, F32)))
    gate_value, up_value, hidden_delta = totals

    sigmoid_gate = jax.nn.sigmoid(gate_value)
    hidden = (gate_value * sigmoid_gate * up_value).astype(BF)
    gate_delta = (
        hidden_delta * up_value * sigmoid_gate * (1.0 + gate_value * (1.0 - sigmoid_gate))
    ).astype(BF)
    up_delta = (hidden_delta * gate_value * sigmoid_gate).astype(BF)

    hidden = gather_rows(hidden, DOWN)
    gate_delta = gather_rows(gate_delta, GATE)
    up_delta = gather_rows(up_delta, UP)

    def finish(tail, orders, dims, values, weights, weights_o):
        away = output(tail, orders, dims, BF, meta, values, weights_o, features)
        got = swap(away, "c")
        total = output(tail, orders, dims, F32, meta, values, weights, features) + got.astype(F32)
        return reduce_rest(total, tail, swap_tensor, (BF, BF, BF)).astype(BF)

    ffn_output = finish("aby", (DOWN,), (1, 0), (hidden,), (down_w,), (down_o,))
    input_gradient = finish(
        "bay", (GATE, UP), (1, 1), (gate_delta, up_delta), (gate_w, up_w), (gate_o, up_o)
    )

    away = gradients(meta, tokens_o, cotangent_o, hidden, gate_delta, up_delta)
    theirs = [swap(v, "c") for v in away]
    mine = gradients(meta, tokens, cotangent, hidden, gate_delta, up_delta)
    grads = call(
        functools.partial(scatter_kernel, owned),
        (
            shape(features, owned * BLK),
            shape(features, owned * BLK),
            shape(owned * BLK, features),
        ),
        [SM, SM] + [VM] * 6,
        (meta, kept_blocks, *mine, *theirs),
        [
            pltpu.VMEM((features, BLK), BF),
            pltpu.VMEM((BLK, features), BF),
            pltpu.SemaphoreType.DMA((3,)),
        ],
        nbytes=10 * 2**20,
        out_specs=(ANY, ANY, ANY),
    )
    return (ffn_output, input_gradient, *grads)


def solution(mesh):
    in_specs = (
        P(None, "dp"),
        P(None, "dp"),
        P("dp", "tensor"),
        P("dp", "tensor"),
        P("tensor", "dp"),
        P(),
    )
    out_specs = (
        P("tensor", "dp"),
        P("tensor", "dp"),
        P("dp", "tensor"),
        P("dp", "tensor"),
        P("tensor", "dp"),
    )
    return jax.shard_map(body, mesh=mesh, in_specs=in_specs, out_specs=out_specs, check_vma=False)
```
